32 devices in a mesh: slab: 8 (over z, core), row: 4 (over y, x).
Axes of the slice: x: 2, y: 2, z: 4, core: 2. Of those that a mesh axis runs over, the one named last changes fastest.
Arguments:
- propagator_matrices: float32 [16, 512, 512], P('slab', 'row'), may hold values from -1 to 2
- gain: float32 [512, 128], replicated, may hold values from -0.0546875 to 0.0546875
- obs_matrix: float32 [128, 512], replicated, may hold values from -0.25 to 0.25
- observations: float32 [16, 128], P('slab'), may hold values from -6 to 6
- present: int32 [16], P('slab'), may hold values 0 or 1
- initial: float32 [512], replicated, may hold values from -6 to 6
- smoother_gain: float32 [512, 512], P('row'), may hold values from -1 to 2
Outputs:
- filtered: float32 [16, 512], P('slab')
- smoothed: float32 [16, 512], P('slab')
The draws below stay inside these ranges and needn't reach their ends.
All inputs are finite; a program needn't handle non-finite values. No bound on the sum of `present` on one device may be relied on, other than what follows from the above.
Results may differ from the reference program's by a relative error of at most 0.00015.
Values sent between devices are 32-bit elements; how exact they have to be, the bound alone decides.
No kernel may reach another device: no remote copies, remote signals or barrier semaphores. Data moves between devices by JAX's collectives and lax.ppermute only.
A program may use at most 192 MiB of HBM per device.

```python
import math
import jax
import jax.numpy as jnp
from jax import lax

D = 512
OBS = 128
HORIZON_LENGTH = 16


def noise_part(key, array_extent):
    values = jnp.clip(jax.random.normal(key, array_extent, jnp.float32), -3.0, 3.0)
    return values * (0.15 / math.sqrt(D))


def draw_propagator_matrices(key, part):
    key_rate = jax.random.fold_in(key, 11)
    key_stretch = jax.random.fold_in(key, 12)
    outage_seed_handle = jax.random.fold_in(key, 13)
    key_noise = jax.random.fold_in(key, 14)
    low = math.log(0.93)
    high = math.log(0.999)
    damping_speeds = jnp.exp(low + (high - low) * jax.random.uniform(key_rate, (D,), jnp.float32))
    widening_scaler = jnp.exp(math.log(0.5) + math.log(4.0) * jax.random.uniform(key_stretch, (HORIZON_LENGTH,), jnp.float32))
    outage_lengths = jnp.where(jax.random.uniform(outage_seed_handle, (HORIZON_LENGTH,), jnp.float32) < 4.0 / HORIZON_LENGTH, 0.6, 1.0)
    principal_coefficients = damping_speeds[None, :] ** widening_scaler[:, None] * outage_lengths[:, None]
    identity = jnp.eye(D, dtype=jnp.float32)
    return principal_coefficients[:, :, None] * identity[None, :, :] + noise_part(key_noise, (HORIZON_LENGTH, D, D))


def draw_smoother_gain(key, part):
    diagonal_random_key = jax.random.fold_in(key, 21)
    key_noise = jax.random.fold_in(key, 22)
    principal_coefficients = jax.random.uniform(diagonal_random_key, (D,), jnp.float32, 0.8, 0.98)
    identity = jnp.eye(D, dtype=jnp.float32)
    return principal_coefficients[:, None] * identity + noise_part(key_noise, (D, D))


def set_ends(drawn, key, least, top_value):
    spot = [jax.random.randint(jax.random.fold_in(key, axis), (), 0, length) for axis, length in enumerate(drawn.shape)]
    widest = drawn.shape.index(max(drawn.shape))
    neighbour = spot[:widest] + [(spot[widest] + 1) % drawn.shape[widest]] + spot[widest + 1:]
    return drawn.at[tuple(spot)].set(least).at[tuple(neighbour)].set(top_value)


def block_scale(own_key, shape, split, low, largest):
    factor_of, own = 1.0, jax.random.fold_in(own_key, 6)
    for position, parts in split:
        heights = jnp.exp(jax.random.uniform(jax.random.fold_in(own, position), (parts,), jnp.float32, low / len(split), largest / len(split)))
        factor_of = factor_of * jnp.repeat(heights, shape[position] // parts).reshape([-1 if axis == position else 1 for axis in range(len(shape))])
    return factor_of


def centred(rng, shape, width, reach, pieces=(), kind=jnp.bfloat16):
    array = jax.random.normal(rng, shape, jnp.float32) * width
    if len(pieces) > 0:
        array = block_scale(rng, shape, pieces, -0.22, 0.18) * array
    return jnp.clip(array, min=-reach, max=reach).astype(kind)


def setup_inputs(seed: int = 0) -> dict:
    seeds = jax.random.split(jax.random.key(seed), 8)
    propagator_matrices = draw_propagator_matrices(jax.random.fold_in(seeds[7], 71), 0)
    gain = centred(seeds[1], (D, OBS), (25 * D) ** -0.5, 0.0546875, (), jnp.float32)
    obs_matrix = centred(seeds[2], (OBS, D), D ** -0.5, 0.25, (), jnp.float32)
    observations = centred(seeds[3], (HORIZON_LENGTH, OBS), 1.0, 6.0, ((0, 8),), jnp.float32)
    present = set_ends((jax.random.randint(seeds[4], (HORIZON_LENGTH,), 0, 2) < 1).astype(jnp.int32), jax.random.fold_in(seeds[4], 1), 0, 1)
    initial = centred(seeds[5], (D,), 1.0, 6.0, (), jnp.float32)
    smoother_gain = draw_smoother_gain(jax.random.fold_in(seeds[7], 71), 0)
    return {"propagator_matrices": propagator_matrices, "gain": gain, "obs_matrix": obs_matrix, "observations": observations, "present": present, "initial": initial, "smoother_gain": smoother_gain}


def reference(propagator_matrices, gain, obs_matrix, observations, present, initial, smoother_gain):
    greatest_accuracy = lax.Precision.HIGHEST
    coupling = jnp.dot(gain, obs_matrix, precision=greatest_accuracy)
    weights = present.astype(jnp.float32)

    def forward(state, inputs):
        matrix, observed, weight = inputs
        pred = jnp.dot(matrix, state, precision=greatest_accuracy)
        innovation = jnp.dot(gain, observed, precision=greatest_accuracy) - jnp.dot(coupling, pred, precision=greatest_accuracy)
        new_state = pred + weight * innovation
        return new_state, (new_state, new_state - pred)

    _, (filtered, correction) = lax.scan(forward, initial, (propagator_matrices, observations, weights))

    def backward(carried, term):
        new_carried = jnp.dot(smoother_gain, carried, precision=greatest_accuracy) + term
        return new_carried, new_carried

    _, carried = lax.scan(backward, jnp.zeros_like(initial), correction, reverse=True)
    smoothed = filtered + carried - correction
    return filtered, smoothed
```

```python
import jax
import jax.numpy as jnp
from jax import lax
from jax.sharding import PartitionSpec as P

AXES = ("slab", "row")
HIGH = lax.Precision.HIGH


def mm(a, b):
    return jnp.dot(a, b, precision=HIGH)


def by(matrix, rows):
    return lax.dot_general(rows, matrix, (((1,), (1,)), ((), ())), precision=HIGH)


def solution(mesh):
    slabs, parts = mesh.shape["slab"], mesh.shape["row"]
    planes = slabs // 2
    every = [(s, r) for s in range(slabs) for r in range(parts)]

    def send(a, target, which=lambda s: True):
        perm = []
        for s, r in every:
            s_to, r_to = target(s, r)
            if which(s) and 0 <= s_to < slabs:
                perm.append((s * parts + r, s_to * parts + r_to))
        return lax.ppermute(a, AXES, perm)

    def other_core(a):
        return send(a, lambda s, r: (s ^ 1, r))

    def row_parts(block):
        if parts != 4:
            gathered = lax.all_gather(block, "row", axis=0)
            return [gathered[i] for i in range(parts)]
        half = block.shape[0] // 2
        place = lax.axis_index("row")
        from_x = send(block, lambda s, r: (s, r ^ 1))
        from_y = send(block, lambda s, r: (s, r ^ 2))
        far = lax.concatenate(
            [
                send(from_y[:half], lambda s, r: (s, r ^ 1)),
                send(from_x[half:], lambda s, r: (s, r ^ 2)),
            ],
            0,
        )
        x_bit, y_bit = (place & 1) == 1, (place & 2) == 2
        near_0, near_1 = jnp.where(x_bit, from_x, block), jnp.where(x_bit, block, from_x)
        off_0, off_1 = jnp.where(x_bit, far, from_y), jnp.where(x_bit, from_y, far)
        return [
            jnp.where(y_bit, off_0, near_0),
            jnp.where(y_bit, off_1, near_1),
            jnp.where(y_bit, near_0, off_0),
            jnp.where(y_bit, near_1, off_1),
        ]

    def on_device(propagator_matrices, gain, obs_matrix, observations, present, initial, smoother_gain):
        epochs, part_rows, width = propagator_matrices.shape
        place = lax.axis_index("slab")
        plane, odd = place // 2, place % 2 == 1
        weights = present.astype(jnp.float32)
        drive = weights[:, None] * by(gain, observations)
        half = part_rows // 2
        own_half = lax.dynamic_slice_in_dim(smoother_gain, (place % 2) * half, half, 0)
        block = lax.concatenate([propagator_matrices[e] for e in range(epochs)] + [own_half], 0)
        pieces = row_parts(block)
        full = [
            lax.concatenate([p[e * part_rows : (e + 1) * part_rows] for p in pieces], 0)
            for e in range(epochs)
        ]
        smoother_half = jnp.stack([p[epochs * part_rows :] for p in pieces], 0)

        maps, offsets = [], []
        for e in range(epochs):
            step_map = full[e] - weights[e] * mm(gain, mm(obs_matrix, full[e]))
            if e == 0:
                maps.append(step_map)
                offsets.append(drive[0:1])
            else:
                maps.append(mm(step_map, maps[-1]))
                offsets.append(by(step_map, offsets[-1]) + drive[e : e + 1])

        slab_map = lax.concatenate([maps[-1], jnp.pad(offsets[-1], ((0, 7), (0, 0)))], 0)
        else_map = other_core(slab_map)
        first = jnp.where(odd, else_map, slab_map)
        second = jnp.where(odd, slab_map, else_map)
        first_map, first_offset = first[:width], first[width : width + 1]
        second_map, second_offset = second[:width], second[width : width + 1]
        plane_map = mm(second_map, first_map)
        plane_offset = by(second_map, first_offset) + second_offset

        state = initial[None, :]
        for k in range(planes - 1):
            ahead = by(plane_map, state) + plane_offset
            received = send(ahead, lambda s, r: (s + 2, r), lambda s: s // 2 == k)
            state = jnp.where(plane == k + 1, received, state)

        middle = by(first_map, state) + first_offset
        state = jnp.where(odd, middle, state)
        filtered, correction = [], []
        before = state
        for e in range(epochs):
            pred = by(full[e], before)
            before = by(maps[e], state) + offsets[e]
            filtered.append(before)
            correction.append(before - pred)
        filtered = lax.concatenate(filtered, 0)
        correction = lax.concatenate(correction, 0)

        other = other_core(correction)
        own = lax.concatenate(
            [jnp.where(odd, other, correction), jnp.where(odd, correction, other)], 0
        )
        smoother_half, own = lax.optimization_barrier((smoother_half, own))
        terms = [own]
        for k in range(1, planes):
            terms.append(send(own, lambda s, r: (s - 2 * k, r)))

        else_half = other_core(smoother_half)
        smoother = jnp.stack(
            [
                jnp.where(odd, else_half, smoother_half),
                jnp.where(odd, smoother_half, else_half),
            ],
            1,
        ).reshape(width, width)
        count = 2 * epochs * planes
        powers = [smoother]
        while 2 ** len(powers) < count:
            powers.append(mm(powers[-1], powers[-1]))

        carried = lax.concatenate(terms, 0)
        for i, power in enumerate(powers):
            later = jnp.pad(carried[2**i :], ((0, 2**i), (0, 0)))
            carried = carried + by(power, later)
        carried = jnp.where(odd, carried[epochs : 2 * epochs], carried[:epochs])
        return (filtered, filtered + carried - correction)

    placed = (P("slab", "row", None), P(), P(), P("slab", None), P("slab"), P(), P("row", None))
    return jax.shard_map(
        on_device,
        mesh=mesh,
        in_specs=placed,
        out_specs=(P("slab", None), P("slab", None)),
        check_vma=False,
    )
```

```python
import jax
import jax.numpy as jnp
from jax import lax
from jax.sharding import PartitionSpec as P

AXES = ("slab", "row")
HIGH = lax.Precision.HIGH


def mm(a, b):
    return jnp.dot(a, b, precision=HIGH)


def by(matrix, rows):
    return lax.dot_general(rows, matrix, (((1,), (1,)), ((), ())), precision=HIGH)


def in_order(pieces, place):
    bit = 1
    while bit < len(pieces):
        crossed = (place & bit) != 0
        pieces = [jnp.where(crossed, pieces[i ^ bit], pieces[i]) for i in range(len(pieces))]
        bit *= 2
    return pieces


def after(value, *others):
    return lax.optimization_barrier((value, others))[0]


def solution(mesh):
    slabs, parts = mesh.shape["slab"], mesh.shape["row"]
    planes = slabs // 2
    every = [(s, r) for s in range(slabs) for r in range(parts)]

    def send(a, target, which=lambda s: True):
        perm = []
        for s, r in every:
            s_to, r_to = target(s, r)
            if which(s) and 0 <= s_to < slabs:
                perm.append((s * parts + r, s_to * parts + r_to))
        return lax.ppermute(a, AXES, perm)

    def other_core(a):
        return send(a, lambda s, r: (s ^ 1, r))

    def along(a, bit):
        return send(a, lambda s, r: (s, r ^ bit))

    def over_planes(a):
        return [a] + [send(a, lambda s, r: (s ^ (2 * k), r)) for k in range(1, planes)]

    def on_device(propagator_matrices, gain, obs_matrix, observations, present, initial, smoother_gain):
        epochs, part_rows, width = propagator_matrices.shape
        place, part = lax.axis_index("slab"), lax.axis_index("row")
        plane, odd = place // 2, place % 2 == 1

        share = part_rows // slabs
        own_share = lax.dynamic_slice_in_dim(smoother_gain, place * share, share, 0)

        if parts == 4:
            from_x, from_y = along(propagator_matrices, 1), along(propagator_matrices, 2)
            shares = [own_share] + [along(own_share, bit) for bit in (1, 2, 3)]
            shares = jnp.stack(in_order(shares, part), 0)
            plane_shares = over_planes(shares)
            mid = epochs // 2
            next_x, next_y = after((from_x[mid:], from_y[:mid]), shares)
            far = lax.concatenate([along(next_y, 1), along(next_x, 2)], 0)
            plane_shares, far = lax.optimization_barrier((plane_shares, far))
            pieces = [propagator_matrices, from_x, from_y, far]
            full = lax.concatenate(in_order(pieces, part), 1)
        else:
            full = lax.all_gather(propagator_matrices, "row", axis=1, tiled=True)
            plane_shares = over_planes(lax.all_gather(own_share, "row", axis=0))

        weights = present.astype(jnp.float32)
        drive = weights[:, None] * by(gain, observations)
        taken = [-weights[e] * gain for e in range(epochs)]
        unit = jnp.eye(width, dtype=jnp.float32)
        update = [unit + mm(taken[e], obs_matrix) for e in range(epochs)]

        reach, maps = [], []
        for e in range(epochs):
            reach.append(mm(full[e], maps[-1]) if e else full[e])
            maps.append(mm(update[e], reach[e]))
        slab_map = maps[-1]
        else_map = other_core(slab_map)

        reach = after(reach, slab_map)
        offsets, seen, seen_0 = [], [], []
        for e in range(epochs):
            if e == 0:
                seen_0.append(jnp.zeros((1, obs_matrix.shape[0]), jnp.float32))
                offsets.append(drive[0:1])
            else:
                reach_0 = by(full[e], offsets[-1])
                seen_0.append(by(obs_matrix, reach_0))
                offsets.append(reach_0 + by(taken[e], seen_0[e]) + drive[e : e + 1])
            seen.append(mm(obs_matrix, reach[e]))
        slab_offset = offsets[-1]

        else_offset = other_core(slab_offset)
        plane_map = mm(jnp.where(odd, slab_map, else_map), jnp.where(odd, else_map, slab_map))
        plane_offset = jnp.where(
            odd, by(slab_map, else_offset) + slab_offset, by(else_map, slab_offset) + else_offset
        )

        state = initial[None, :]
        for k in range(planes - 1):
            ahead = by(plane_map, state) + plane_offset
            received = send(ahead, lambda s, r: (s + 2, r), lambda s: s // 2 == k)
            state = jnp.where(plane == k + 1, received, state)

        state = jnp.where(odd, by(else_map, state) + else_offset, state)
        correction = lax.concatenate(
            [
                by(taken[e], by(seen[e], state) + seen_0[e]) + drive[e : e + 1]
                for e in range(epochs)
            ],
            0,
        )
        other = other_core(correction)
        own = lax.concatenate(
            [jnp.where(odd, other, correction), jnp.where(odd, correction, other)], 0
        )
        terms = [own]
        for k in range(1, planes):
            terms.append(send(own, lambda s, r: (s - 2 * k, r)))

        state = after(state, own)
        filtered = lax.concatenate([by(maps[e], state) + offsets[e] for e in range(epochs)], 0)

        mine = after(jnp.stack(in_order(plane_shares, plane), 0), own)
        theirs = other_core(mine)
        smoother = jnp.stack(in_order([mine, theirs], place % 2), 1)
        smoother = smoother.transpose(2, 0, 1, 3, 4).reshape(width, width)
        count = 2 * epochs * planes
        powers = [smoother]
        while 2 ** len(powers) < count:
            powers.append(mm(powers[-1], powers[-1]))
        terms, powers = lax.optimization_barrier((terms, powers))

        carried = lax.concatenate(terms, 0)
        for i, power in enumerate(powers):
            later = jnp.pad(carried[2**i :], ((0, 2**i), (0, 0)))
            carried = carried + by(power, later)
        carried = jnp.where(odd, carried[epochs : 2 * epochs], carried[:epochs])
        return (filtered, filtered + carried - correction)

    placed = (P("slab", "row", None), P(), P(), P("slab", None), P("slab"), P(), P("row", None))
    return jax.shard_map(
        on_device,
        mesh=mesh,
        in_specs=placed,
        out_specs=(P("slab", None), P("slab", None)),
        check_vma=False,
    )
```

```python
import jax
import jax.numpy as jnp
from jax import lax
from jax.sharding import PartitionSpec as P

AXES = ("slab", "row")
HIGH = lax.Precision.HIGH


def mm(a, b):
    return jnp.dot(a, b, precision=HIGH)


def by(matrix, rows):
    return lax.dot_general(rows, matrix, (((1,), (1,)), ((), ())), precision=HIGH)


def in_order(pieces, place):
    bit = 1
    while bit < len(pieces):
        crossed = (place & bit) != 0
        pieces = [jnp.where(crossed, pieces[i ^ bit], pieces[i]) for i in range(len(pieces))]
        bit *= 2
    return pieces


def after(value, *others):
    return lax.optimization_barrier((value, others))[0]


def solution(mesh):
    slabs, parts = mesh.shape["slab"], mesh.shape["row"]
    planes = slabs // 2
    every = [(s, r) for s in range(slabs) for r in range(parts)]

    def send(a, target, which=lambda s: True):
        perm = []
        for s, r in every:
            s_to, r_to = target(s, r)
            if which(s) and 0 <= s_to < slabs:
                perm.append((s * parts + r, s_to * parts + r_to))
        return lax.ppermute(a, AXES, perm)

    def other_core(a):
        return send(a, lambda s, r: (s ^ 1, r))

    def along(a, bit):
        return send(a, lambda s, r: (s, r ^ bit))

    def on_device(propagator_matrices, gain, obs_matrix, observations, present, initial, smoother_gain):
        epochs, part_rows, width = propagator_matrices.shape
        place, part = lax.axis_index("slab"), lax.axis_index("row")
        plane, odd = place // 2, place % 2 == 1

        weights = present.astype(jnp.float32)
        drive = weights[:, None] * by(gain, observations)
        taken = [-weights[e] * gain for e in range(epochs)]
        unit = jnp.eye(width, dtype=jnp.float32)
        update = [unit + mm(taken[e], obs_matrix) for e in range(epochs)]

        share = part_rows // 4
        own_share = lax.dynamic_slice_in_dim(smoother_gain, place % 4 * share, share, 0)
        own_share = after(own_share, update)

        if parts == 4:
            from_x, from_y = along(propagator_matrices, 1), along(propagator_matrices, 2)
            shares = [own_share] + [along(own_share, bit) for bit in (1, 2, 3)]
            shares = jnp.stack(in_order(shares, part), 0)
            mid = epochs // 2
            next_x, next_y = after((from_x[mid:], from_y[:mid]), shares)
            far = lax.concatenate([along(next_y, 1), along(next_x, 2)], 0)
            pieces = [propagator_matrices, from_x, from_y, far]
            full = lax.concatenate(in_order(pieces, part), 1)
        else:
            full = lax.all_gather(propagator_matrices, "row", axis=1, tiled=True)
            shares = lax.all_gather(own_share, "row", axis=0)
        next_shares = send(shares, lambda s, r: (s ^ 2, r))

        reach, maps = [], []
        for e in range(epochs):
            reach.append(mm(full[e], maps[-1]) if e else full[e])
            maps.append(mm(update[e], reach[e]))
        slab_map, shares, next_shares = lax.optimization_barrier((maps[-1], shares, next_shares))
        maps[-1] = slab_map
        else_map = other_core(slab_map)
        mine = jnp.stack(in_order([shares, next_shares], plane % 2), 0)
        theirs = other_core(mine)

        offsets, reach_0 = [drive[0:1]], [None]
        for e in range(1, epochs):
            reach_0.append(by(full[e], offsets[-1]))
            offsets.append(by(update[e], reach_0[e]) + drive[e : e + 1])
        slab_offset = offsets[-1]

        else_offset = other_core(slab_offset)
        plane_map = mm(jnp.where(odd, slab_map, else_map), jnp.where(odd, else_map, slab_map))
        plane_offset = jnp.where(
            odd, by(slab_map, else_offset) + slab_offset, by(else_map, slab_offset) + else_offset
        )

        powers, seen, seen_0 = [], [], []
        count = 2 * epochs * planes

        def smoother_rows(ahead):
            smoother = jnp.stack(in_order(after([mine, theirs], ahead), place % 2), 1)
            powers.append(smoother.transpose(2, 0, 1, 3, 4).reshape(width, width))
            powers.append(mm(powers[0], powers[0]))

        def smoother_powers(ahead):
            powers[-1] = after(powers[-1], ahead)
            while 2 ** len(powers) < count:
                powers.append(mm(powers[-1], powers[-1]))

        def observed_maps(ahead):
            for e, a in enumerate(after(reach, ahead)):
                seen.append(mm(obs_matrix, a))
                seen_0.append(by(obs_matrix, reach_0[e]) if e else jnp.zeros((1, obs_matrix.shape[0])))

        works = [smoother_rows, smoother_powers, observed_maps]
        state = initial[None, :]
        for k in range(planes - 1):
            ahead = by(plane_map, state) + plane_offset
            received = send(ahead, lambda s, r: (s + 2, r), lambda s: s // 2 == k)
            if works:
                works.pop(0)(ahead)
                received, powers, seen, seen_0 = lax.optimization_barrier(
                    (received, powers, seen, seen_0)
                )
            state = jnp.where(plane == k + 1, received, state)
        for work in works:
            work(state)

        state = jnp.where(odd, by(else_map, state) + else_offset, state)
        correction = lax.concatenate(
            [
                by(taken[e], by(seen[e], state) + seen_0[e]) + drive[e : e + 1]
                for e in range(epochs)
            ],
            0,
        )
        other = other_core(correction)
        own = lax.concatenate(
            [jnp.where(odd, other, correction), jnp.where(odd, correction, other)], 0
        )
        terms = [own]
        for k in range(1, planes):
            terms.append(send(own, lambda s, r: (s - 2 * k, r)))

        state = after(state, own)
        filtered = lax.concatenate([by(maps[e], state) + offsets[e] for e in range(epochs)], 0)

        carried = lax.concatenate(terms, 0)
        for i, power in enumerate(powers):
            later = jnp.pad(carried[2**i :], ((0, 2**i), (0, 0)))
            carried = carried + by(power, later)
        carried = jnp.where(odd, carried[epochs : 2 * epochs], carried[:epochs])
        return (filtered, filtered + carried - correction)

    placed = (P("slab", "row", None), P(), P(), P("slab", None), P("slab"), P(), P("row", None))
    return jax.shard_map(
        on_device,
        mesh=mesh,
        in_specs=placed,
        out_specs=(P("slab", None), P("slab", None)),
        check_vma=False,
    )
```

```python
import jax
import jax.numpy as jnp
from jax import lax
from jax.sharding import PartitionSpec as P

AXES = ("slab", "row")
HIGH = lax.Precision.HIGH


def mm(a, b):
    return jnp.dot(a, b, precision=HIGH)


def by(matrix, rows):
    return lax.dot_general(rows, matrix, (((1,), (1,)), ((), ())), precision=HIGH)


def in_order(pieces, place):
    bit = 1
    while bit < len(pieces):
        crossed = (place & bit) != 0
        pieces = [jnp.where(crossed, pieces[i ^ bit], pieces[i]) for i in range(len(pieces))]
        bit *= 2
    return pieces


def after(value, *others):
    return lax.optimization_barrier((value, others))[0]


def solution(mesh):
    slabs, parts = mesh.shape["slab"], mesh.shape["row"]
    planes = slabs // 2
    every = [(s, r) for s in range(slabs) for r in range(parts)]

    def send(a, target, which=lambda s: True):
        perm = []
        for s, r in every:
            s_to, r_to = target(s, r)
            if which(s) and 0 <= s_to < slabs:
                perm.append((s * parts + r, s_to * parts + r_to))
        return lax.ppermute(a, AXES, perm)

    def other_core(a):
        return send(a, lambda s, r: (s ^ 1, r))

    def along(a, bit):
        return send(a, lambda s, r: (s, r ^ bit))

    def on_device(propagator_matrices, gain, obs_matrix, observations, present, initial, smoother_gain):
        epochs, part_rows, width = propagator_matrices.shape
        place, part = lax.axis_index("slab"), lax.axis_index("row")
        plane, odd = place // 2, place % 2 == 1

        weights = present.astype(jnp.float32)
        drive = weights[:, None] * by(gain, observations)
        taken = [-weights[e] * gain for e in range(epochs)]
        unit = jnp.eye(width, dtype=jnp.float32)
        update = [unit + mm(taken[e], obs_matrix) for e in range(epochs)]

        share = part_rows // 4
        own_share = lax.dynamic_slice_in_dim(smoother_gain, place % 4 * share, share, 0)
        own_share = after(own_share, update)

        if parts == 4:
            from_x, from_y = along(propagator_matrices, 1), along(propagator_matrices, 2)
            shares = [own_share] + [along(own_share, bit) for bit in (1, 2, 3)]
            shares = jnp.stack(in_order(shares, part), 0)
            mid = epochs // 2
            far = lax.concatenate([along(from_y[:mid], 1), along(from_x[mid:], 2)], 0)
            far = after(far, shares)
            pieces = [propagator_matrices, from_x, from_y, far]
            full = lax.concatenate(in_order(pieces, part), 1)
        else:
            full = lax.all_gather(propagator_matrices, "row", axis=1, tiled=True)
            shares = lax.all_gather(own_share, "row", axis=0)
        next_shares = send(shares, lambda s, r: (s ^ 2, r))

        reach, maps = [], []
        for e in range(epochs):
            reach.append(mm(full[e], maps[-1]) if e else full[e])
            maps.append(mm(update[e], reach[e]))
        slab_map, shares, next_shares = lax.optimization_barrier((maps[-1], shares, next_shares))
        maps[-1] = slab_map
        else_map = other_core(slab_map)
        mine = jnp.stack(in_order([shares, next_shares], plane % 2), 0)
        theirs = other_core(mine)

        offsets, reach_0 = [drive[0:1]], [None]
        for e in range(1, epochs):
            reach_0.append(by(full[e], offsets[-1]))
            offsets.append(by(update[e], reach_0[e]) + drive[e : e + 1])
        slab_offset = offsets[-1]

        else_offset = other_core(slab_offset)
        plane_map = mm(jnp.where(odd, slab_map, else_map), jnp.where(odd, else_map, slab_map))
        plane_offset = jnp.where(
            odd, by(slab_map, else_offset) + slab_offset, by(else_map, slab_offset) + else_offset
        )

        powers, seen, seen_0 = [], [], []
        count = 2 * epochs * planes

        def smoother_rows(ahead):
            smoother = jnp.stack(in_order(after([mine, theirs], ahead), place % 2), 1)
            powers.append(smoother.transpose(2, 0, 1, 3, 4).reshape(width, width))
            powers.append(mm(powers[0], powers[0]))

        def smoother_powers(ahead):
            powers[-1] = after(powers[-1], ahead)
            while 2 ** len(powers) < count:
                powers.append(mm(powers[-1], powers[-1]))

        def observed_maps(ahead):
            for e, a in enumerate(after(reach, ahead)):
                seen.append(mm(obs_matrix, a))
                seen_0.append(by(obs_matrix, reach_0[e]) if e else jnp.zeros((1, obs_matrix.shape[0])))

        works = [smoother_rows, smoother_powers, observed_maps]
        state = initial[None, :]
        for k in range(planes - 1):
            ahead = by(plane_map, state) + plane_offset
            received = send(ahead, lambda s, r: (s + 2, r), lambda s: s // 2 == k)
            if works:
                works.pop(0)(ahead)
                received, powers, seen, seen_0 = lax.optimization_barrier(
                    (received, powers, seen, seen_0)
                )
            state = jnp.where(plane == k + 1, received, state)
        for work in works:
            work(state)

        state = jnp.where(odd, by(else_map, state) + else_offset, state)
        correction = lax.concatenate(
            [
                by(taken[e], by(seen[e], state) + seen_0[e]) + drive[e : e + 1]
                for e in range(epochs)
            ],
            0,
        )
        other = other_core(correction)
        own = lax.concatenate(
            [jnp.where(odd, other, correction), jnp.where(odd, correction, other)], 0
        )
        terms = [own]
        for k in range(1, planes):
            terms.append(send(own, lambda s, r: (s - 2 * k, r)))

        state = after(state, own)
        filtered = lax.concatenate([by(maps[e], state) + offsets[e] for e in range(epochs)], 0)

        carried = lax.concatenate(terms, 0)
        for i, power in enumerate(powers):
            later = jnp.pad(carried[2**i :], ((0, 2**i), (0, 0)))
            carried = carried + by(power, later)
        carried = jnp.where(odd, carried[epochs : 2 * epochs], carried[:epochs])
        return (filtered, filtered + carried - correction)

    placed = (P("slab", "row", None), P(), P(), P("slab", None), P("slab"), P(), P("row", None))
    return jax.shard_map(
        on_device,
        mesh=mesh,
        in_specs=placed,
        out_specs=(P("slab", None), P("slab", None)),
        check_vma=False,
    )
```

```python
import jax
import jax.numpy as jnp
from jax import lax
from jax.sharding import PartitionSpec as P

AXES = ("slab", "row")
HIGH = lax.Precision.HIGH


def mm(a, b):
    return jnp.dot(a, b, precision=HIGH)


def by(matrix, rows):
    return lax.dot_general(rows, matrix, (((1,), (1,)), ((), ())), precision=HIGH)


def in_order(pieces, place):
    bit = 1
    while bit < len(pieces):
        crossed = (place & bit) != 0
        pieces = [jnp.where(crossed, pieces[i ^ bit], pieces[i]) for i in range(len(pieces))]
        bit *= 2
    return pieces


def after(value, *others):
    return lax.optimization_barrier((value, others))[0]


def solution(mesh):
    slabs, parts = mesh.shape["slab"], mesh.shape["row"]
    planes = slabs // 2
    every = [(s, r) for s in range(slabs) for r in range(parts)]

    def send(a, target, which=lambda s: True):
        perm = []
        for s, r in every:
            s_to, r_to = target(s, r)
            if which(s) and 0 <= s_to < slabs:
                perm.append((s * parts + r, s_to * parts + r_to))
        return lax.ppermute(a, AXES, perm)

    def other_core(a):
        return send(a, lambda s, r: (s ^ 1, r))

    def along(a, bit):
        return send(a, lambda s, r: (s, r ^ bit))

    def on_device(propagator_matrices, gain, obs_matrix, observations, present, initial, smoother_gain):
        epochs, part_rows, width = propagator_matrices.shape
        place, part = lax.axis_index("slab"), lax.axis_index("row")
        plane, odd = place // 2, place % 2 == 1

        weights = present.astype(jnp.float32)
        drive = weights[:, None] * by(gain, observations)
        taken = [-weights[e] * gain for e in range(epochs)]

        share = part_rows // 4
        own_share = lax.dynamic_slice_in_dim(smoother_gain, place % 4 * share, share, 0)
        own_share = after(own_share, drive)

        if parts == 4:
            from_x, from_y = along(propagator_matrices, 1), along(propagator_matrices, 2)
            shares = [own_share] + [along(own_share, bit) for bit in (1, 2, 3)]
            shares = jnp.stack(in_order(shares, part), 0)
            mid = epochs // 2
            far = lax.concatenate([along(from_y[:mid], 1), along(from_x[mid:], 2)], 0)
            far = after(far, shares)
            pieces = [propagator_matrices, from_x, from_y, far]
            full = lax.concatenate(in_order(pieces, part), 1)
        else:
            full = lax.all_gather(propagator_matrices, "row", axis=1, tiled=True)
            shares = lax.all_gather(own_share, "row", axis=0)
        next_shares = send(shares, lambda s, r: (s ^ 2, r))

        maps, seen = [], []
        for e in range(epochs):
            reach = mm(full[e], maps[-1]) if e else full[e]
            seen.append(mm(obs_matrix, reach))
            maps.append(reach + mm(taken[e], seen[e]))
        slab_map, shares, next_shares = lax.optimization_barrier((maps[-1], shares, next_shares))
        maps[-1] = slab_map
        else_map = other_core(slab_map)
        mine = jnp.stack(in_order([shares, next_shares], plane % 2), 0)
        theirs = other_core(mine)

        offsets = [after(drive, slab_map)[0:1]]
        seen_0 = [jnp.zeros((1, obs_matrix.shape[0]), jnp.float32)]
        for e in range(1, epochs):
            reach_0 = by(full[e], offsets[-1])
            seen_0.append(by(obs_matrix, reach_0))
            offsets.append(reach_0 + by(taken[e], seen_0[e]) + drive[e : e + 1])
        slab_offset = offsets[-1]

        else_offset = other_core(slab_offset)
        plane_map = mm(jnp.where(odd, slab_map, else_map), jnp.where(odd, else_map, slab_map))
        last_offset = by(slab_map, else_offset) + slab_offset
        else_last = after(other_core(last_offset), plane_map)
        plane_offset = jnp.where(odd, last_offset, else_last)

        powers = []
        count = 2 * epochs * planes

        def first_work(ahead):
            smoother = jnp.stack(in_order(after([mine, theirs], ahead), place % 2), 1)
            powers.append(smoother.transpose(2, 0, 1, 3, 4).reshape(width, width))
            powers.append(mm(powers[0], powers[0]))
            maps_0, base = after((seen, seen_0), ahead)
            seen[:] = [
                lax.concatenate([-weights[e] * maps_0[e] for e in range(epochs)], 0),
                weights[:, None] * (observations - lax.concatenate(base, 0)),
            ]

        def second_work(ahead):
            powers[-1], seen[:] = after((powers[-1], seen), ahead)
            powers.append(mm(powers[-1], powers[-1]))
            moved = [mm(seen[0], else_map), by(seen[0], else_offset).reshape(seen[1].shape) + seen[1]]
            seen[:] = [jnp.where(odd, a, b) for a, b in zip(moved, seen)]

        def third_work(ahead):
            powers[-1], seen[:] = after((powers[-1], seen), ahead)
            seen[:] = [
                lax.concatenate(in_order([a, other_core(a)], place % 2), 0) for a in seen
            ]
            while 2 ** len(powers) < count:
                powers.append(mm(powers[-1], powers[-1]))

        works = [first_work, second_work, third_work]
        state = initial[None, :]
        for k in range(planes - 1):
            ahead = by(plane_map, state) + plane_offset
            received = send(ahead, lambda s, r: (s + 2, r), lambda s: s // 2 == k)
            if works:
                works.pop(0)(ahead)
                received, powers, seen = lax.optimization_barrier((received, powers, seen))
            state = jnp.where(plane == k + 1, received, state)
        for work in works:
            work(state)

        innovations = by(seen[0], state).reshape(seen[1].shape) + seen[1]
        own = by(gain, innovations)
        terms = [own]
        for k in range(1, planes):
            terms.append(send(own, lambda s, r: (s - 2 * k, r)))

        state = after(state, own)
        state = jnp.where(odd, by(else_map, state) + else_offset, state)
        correction = jnp.where(odd, own[epochs:], own[:epochs])
        filtered = lax.concatenate([by(maps[e], state) + offsets[e] for e in range(epochs)], 0)

        carried = lax.concatenate(terms, 0)
        for i, power in enumerate(powers):
            later = jnp.pad(carried[2**i :], ((0, 2**i), (0, 0)))
            carried = carried + by(power, later)
        carried = jnp.where(odd, carried[epochs : 2 * epochs], carried[:epochs])
        return (filtered, filtered + carried - correction)

    placed = (P("slab", "row", None), P(), P(), P("slab", None), P("slab"), P(), P("row", None))
    return jax.shard_map(
        on_device,
        mesh=mesh,
        in_specs=placed,
        out_specs=(P("slab", None), P("slab", None)),
        check_vma=False,
    )
```

```python
import jax
import jax.numpy as jnp
from jax import lax
from jax.experimental.layout import Layout, with_layout_constraint
from jax.sharding import PartitionSpec as P

AXES = ("slab", "row")
HIGH = lax.Precision.HIGH


def mm(a, b):
    return jnp.dot(a, b, precision=HIGH)


def by(matrix, rows):
    return lax.dot_general(rows, matrix, (((1,), (1,)), ((), ())), precision=HIGH)


def rowwise(a):
    return with_layout_constraint(a, Layout((0, 1)))


def in_order(pieces, place):
    bit = 1
    while bit < len(pieces):
        crossed = (place & bit) != 0
        pieces = [jnp.where(crossed, pieces[i ^ bit], pieces[i]) for i in range(len(pieces))]
        bit *= 2
    return pieces


def after(value, *others):
    return lax.optimization_barrier((value, others))[0]


def solution(mesh):
    slabs, parts = mesh.shape["slab"], mesh.shape["row"]
    planes = slabs // 2
    every = [(s, r) for s in range(slabs) for r in range(parts)]

    def send(a, target, which=lambda s: True):
        perm = []
        for s, r in every:
            s_to, r_to = target(s, r)
            if which(s) and 0 <= s_to < slabs:
                perm.append((s * parts + r, s_to * parts + r_to))
        return lax.ppermute(a, AXES, perm)

    def other_core(a):
        return send(a, lambda s, r: (s ^ 1, r))

    def along(a, bit):
        return send(a, lambda s, r: (s, r ^ bit))

    def on_device(propagator_matrices, gain, obs_matrix, observations, present, initial, smoother_gain):
        epochs, part_rows, width = propagator_matrices.shape
        place, part = lax.axis_index("slab"), lax.axis_index("row")
        plane, odd = place // 2, place % 2 == 1

        weights = present.astype(jnp.float32)
        drive = weights[:, None] * by(gain, observations)
        taken = [-weights[e] * gain for e in range(epochs)]

        share = part_rows // 4
        own_share = lax.dynamic_slice_in_dim(smoother_gain, place % 4 * share, share, 0)
        own_share = after(own_share, drive)

        if parts == 4:
            from_x, from_y = along(propagator_matrices, 1), along(propagator_matrices, 2)
            shares = [own_share] + [along(own_share, bit) for bit in (1, 2, 3)]
            shares = jnp.stack(in_order(shares, part), 0)
            mid = epochs // 2
            far = lax.concatenate([along(from_y[:mid], 1), along(from_x[mid:], 2)], 0)
            far = after(far, shares)
            pieces = [propagator_matrices, from_x, from_y, far]
            full = lax.concatenate(in_order(pieces, part), 1)
        else:
            full = lax.all_gather(propagator_matrices, "row", axis=1, tiled=True)
            shares = lax.all_gather(own_share, "row", axis=0)
        next_shares = send(shares, lambda s, r: (s ^ 2, r))

        maps, seen = [], []
        for e in range(epochs):
            reach = mm(full[e], maps[-1]) if e else full[e]
            seen.append(rowwise(mm(obs_matrix, reach)))
            maps.append(reach + mm(taken[e], seen[e]))
        slab_map, shares, next_shares = lax.optimization_barrier((maps[-1], shares, next_shares))
        maps[-1] = slab_map
        else_map = other_core(slab_map)
        mine = jnp.stack(in_order([shares, next_shares], plane % 2), 0)
        theirs = other_core(mine)

        offsets = [after(drive, slab_map)[0:1]]
        seen_0 = [jnp.zeros((1, obs_matrix.shape[0]), jnp.float32)]
        for e in range(1, epochs):
            reach_0 = by(full[e], offsets[-1])
            seen_0.append(by(obs_matrix, reach_0))
            offsets.append(reach_0 + by(taken[e], seen_0[e]) + drive[e : e + 1])
        slab_offset = offsets[-1]

        else_offset = other_core(slab_offset)
        plane_map = mm(jnp.where(odd, slab_map, else_map), jnp.where(odd, else_map, slab_map))
        last_offset = by(slab_map, else_offset) + slab_offset
        else_last = after(other_core(last_offset), plane_map)
        plane_offset = jnp.where(odd, last_offset, else_last)

        powers = []
        count = 2 * epochs * planes

        def first_work(ahead):
            smoother = jnp.stack(in_order(after([mine, theirs], ahead), place % 2), 1)
            powers.append(smoother.transpose(2, 0, 1, 3, 4).reshape(width, width))
            powers.append(mm(powers[0], powers[0]))
            maps_0, base = after((seen, seen_0), ahead)
            seen[:] = [
                lax.concatenate([-weights[e] * maps_0[e] for e in range(epochs)], 0),
                weights[:, None] * (observations - lax.concatenate(base, 0)),
            ]

        def second_work(ahead):
            powers[-1], seen[:] = after((powers[-1], seen), ahead)
            powers.append(mm(powers[-1], powers[-1]))
            moved = [mm(seen[0], else_map), by(seen[0], else_offset).reshape(seen[1].shape) + seen[1]]
            seen[:] = [jnp.where(odd, a, b) for a, b in zip(moved, seen)]

        def third_work(ahead):
            powers[-1], seen[:] = after((powers[-1], seen), ahead)
            seen[:] = [
                lax.concatenate(in_order([a, other_core(a)], place % 2), 0) for a in seen
            ]
            while 2 ** len(powers) < count:
                powers.append(mm(powers[-1], powers[-1]))

        works = [first_work, second_work, third_work]
        state = initial[None, :]
        for k in range(planes - 1):
            ahead = by(plane_map, state) + plane_offset
            received = send(ahead, lambda s, r: (s + 2, r), lambda s: s // 2 == k)
            if works:
                works.pop(0)(ahead)
                received, powers, seen = lax.optimization_barrier((received, powers, seen))
            state = jnp.where(plane == k + 1, received, state)
        for work in works:
            work(state)

        innovations = by(seen[0], state).reshape(seen[1].shape) + seen[1]
        own = by(gain, innovations)
        terms = [own]
        for k in range(1, planes):
            terms.append(send(own, lambda s, r: (s - 2 * k, r)))

        state = after(state, own)
        state = jnp.where(odd, by(else_map, state) + else_offset, state)
        correction = jnp.where(odd, own[epochs:], own[:epochs])
        filtered = lax.concatenate([by(maps[e], state) + offsets[e] for e in range(epochs)], 0)

        carried = lax.concatenate(terms, 0)
        for i, power in enumerate(powers):
            later = jnp.pad(carried[2**i :], ((0, 2**i), (0, 0)))
            carried = carried + by(power, later)
        carried = jnp.where(odd, carried[epochs : 2 * epochs], carried[:epochs])
        return (filtered, filtered + carried - correction)

    placed = (P("slab", "row", None), P(), P(), P("slab", None), P("slab"), P(), P("row", None))
    return jax.shard_map(
        on_device,
        mesh=mesh,
        in_specs=placed,
        out_specs=(P("slab", None), P("slab", None)),
        check_vma=False,
    )
```

```python
import jax
import jax.numpy as jnp
from jax import lax
from jax.experimental.layout import Layout, with_layout_constraint
from jax.sharding import PartitionSpec as P

AXES = ("slab", "row")
HIGH = lax.Precision.HIGH


def mm(a, b):
    return jnp.dot(a, b, precision=HIGH)


def by(matrix, rows):
    return lax.dot_general(rows, matrix, (((1,), (1,)), ((), ())), precision=HIGH)


def rowwise(a):
    return with_layout_constraint(a, Layout((0, 1)))


def in_order(pieces, place):
    bit = 1
    while bit < len(pieces):
        crossed = (place & bit) != 0
        pieces = [jnp.where(crossed, pieces[i ^ bit], pieces[i]) for i in range(len(pieces))]
        bit *= 2
    return pieces


def after(value, *others):
    return lax.optimization_barrier((value, others))[0]


def solution(mesh):
    slabs, parts = mesh.shape["slab"], mesh.shape["row"]
    planes = slabs // 2
    every = [(s, r) for s in range(slabs) for r in range(parts)]

    def send(a, target, which=lambda s: True):
        perm = []
        for s, r in every:
            s_to, r_to = target(s, r)
            if which(s) and 0 <= s_to < slabs:
                perm.append((s * parts + r, s_to * parts + r_to))
        return lax.ppermute(a, AXES, perm)

    def other_core(a):
        return send(a, lambda s, r: (s ^ 1, r))

    def along(a, bit):
        return send(a, lambda s, r: (s, r ^ bit))

    def on_device(propagator_matrices, gain, obs_matrix, observations, present, initial, smoother_gain):
        epochs, part_rows, width = propagator_matrices.shape
        place, part = lax.axis_index("slab"), lax.axis_index("row")
        plane, odd = place // 2, place % 2 == 1

        weights = present.astype(jnp.float32)
        drive = weights[:, None] * by(gain, observations)
        taken = lax.optimization_barrier([-weights[e] * gain for e in range(epochs)])

        share = part_rows // 4
        own_share = lax.dynamic_slice_in_dim(smoother_gain, place % 4 * share, share, 0)
        own_share = after(own_share, drive)

        if parts == 4:
            from_x, from_y = along(propagator_matrices, 1), along(propagator_matrices, 2)
            shares = [own_share] + [along(own_share, bit) for bit in (1, 2, 3)]
            shares = jnp.stack(in_order(shares, part), 0)
            mid = epochs // 2
            far = lax.concatenate([along(from_y[:mid], 1), along(from_x[mid:], 2)], 0)
            far = after(far, shares)
            pieces = [propagator_matrices, from_x, from_y, far]
            full = lax.concatenate(in_order(pieces, part), 1)
        else:
            full = lax.all_gather(propagator_matrices, "row", axis=1, tiled=True)
            shares = lax.all_gather(own_share, "row", axis=0)
        next_shares = send(shares, lambda s, r: (s ^ 2, r))

        maps, seen = [], []
        for e in range(epochs):
            reach = mm(full[e], maps[-1]) if e else full[e]
            seen.append(rowwise(mm(obs_matrix, reach)))
            maps.append(reach + mm(taken[e], seen[e]))
        slab_map, shares, next_shares = lax.optimization_barrier((maps[-1], shares, next_shares))
        maps[-1] = slab_map
        else_map = other_core(slab_map)
        mine = jnp.stack(in_order([shares, next_shares], plane % 2), 0)
        theirs = other_core(mine)

        offsets = [after(drive, slab_map)[0:1]]
        seen_0 = [jnp.zeros((1, obs_matrix.shape[0]), jnp.float32)]
        for e in range(1, epochs):
            reach_0 = by(full[e], offsets[-1])
            seen_0.append(by(obs_matrix, reach_0))
            offsets.append(reach_0 + by(taken[e], seen_0[e]) + drive[e : e + 1])
        slab_offset = offsets[-1]

        else_offset = other_core(slab_offset)
        plane_map = mm(jnp.where(odd, slab_map, else_map), jnp.where(odd, else_map, slab_map))
        last_offset = by(slab_map, else_offset) + slab_offset
        else_last = after(other_core(last_offset), plane_map)
        plane_offset = jnp.where(odd, last_offset, else_last)

        powers = []
        count = 2 * epochs * planes

        def first_work(ahead):
            smoother = jnp.stack(in_order(after([mine, theirs], ahead), place % 2), 1)
            powers.append(smoother.transpose(2, 0, 1, 3, 4).reshape(width, width))
            powers.append(mm(powers[0], powers[0]))
            maps_0, base = after((seen, seen_0), ahead)
            seen[:] = [
                lax.concatenate([-weights[e] * maps_0[e] for e in range(epochs)], 0),
                weights[:, None] * (observations - lax.concatenate(base, 0)),
            ]

        def second_work(ahead):
            powers[-1], seen[:] = after((powers[-1], seen), ahead)
            powers.append(mm(powers[-1], powers[-1]))
            moved = [rowwise(mm(seen[0], else_map)), by(seen[0], else_offset).reshape(seen[1].shape) + seen[1]]
            seen[:] = [jnp.where(odd, a, b) for a, b in zip(moved, seen)]

        def third_work(ahead):
            powers[-1], seen[:] = after((powers[-1], seen), ahead)
            seen[:] = [
                lax.concatenate(in_order([a, other_core(a)], place % 2), 0) for a in seen
            ]
            while 2 ** len(powers) < count:
                powers.append(mm(powers[-1], powers[-1]))

        works = [first_work, second_work, third_work]
        state = initial[None, :]
        for k in range(planes - 1):
            ahead = by(plane_map, state) + plane_offset
            received = send(ahead, lambda s, r: (s + 2, r), lambda s: s // 2 == k)
            if works:
                works.pop(0)(ahead)
                received, powers, seen = lax.optimization_barrier((received, powers, seen))
            state = jnp.where(plane == k + 1, received, state)
        for work in works:
            work(state)

        innovations = by(seen[0], state).reshape(seen[1].shape) + seen[1]
        own = by(gain, innovations)
        terms = [own]
        for k in range(1, planes):
            terms.append(send(own, lambda s, r: (s - 2 * k, r)))

        state = after(state, own)
        state = jnp.where(odd, by(else_map, state) + else_offset, state)
        correction = jnp.where(odd, own[epochs:], own[:epochs])
        filtered = lax.concatenate([by(maps[e], state) + offsets[e] for e in range(epochs)], 0)

        carried = lax.concatenate(terms, 0)
        for i, power in enumerate(powers):
            later = jnp.pad(carried[2**i :], ((0, 2**i), (0, 0)))
            carried = carried + by(power, later)
        carried = jnp.where(odd, carried[epochs : 2 * epochs], carried[:epochs])
        return (filtered, filtered + carried - correction)

    placed = (P("slab", "row", None), P(), P(), P("slab", None), P("slab"), P(), P("row", None))
    return jax.shard_map(
        on_device,
        mesh=mesh,
        in_specs=placed,
        out_specs=(P("slab", None), P("slab", None)),
        check_vma=False,
    )
```

```python
import jax
import jax.numpy as jnp
from jax import lax
from jax.experimental.layout import Layout, with_layout_constraint
from jax.sharding import PartitionSpec as P

AXES = ("slab", "row")
HIGH = lax.Precision.HIGH


def mm(a, b):
    return jnp.dot(a, b, precision=HIGH)


def by(matrix, rows):
    return lax.dot_general(rows, matrix, (((1,), (1,)), ((), ())), precision=HIGH)


def rowwise(a):
    return with_layout_constraint(a, Layout((0, 1)))


def in_order(pieces, place):
    bit = 1
    while bit < len(pieces):
        crossed = (place & bit) != 0
        pieces = [jnp.where(crossed, pieces[i ^ bit], pieces[i]) for i in range(len(pieces))]
        bit *= 2
    return pieces


def after(value, *others):
    return lax.optimization_barrier((value, others))[0]


def solution(mesh):
    slabs, parts = mesh.shape["slab"], mesh.shape["row"]
    planes = slabs // 2
    every = [(s, r) for s in range(slabs) for r in range(parts)]

    def send(a, target, which=lambda s: True):
        perm = []
        for s, r in every:
            s_to, r_to = target(s, r)
            if which(s) and 0 <= s_to < slabs:
                perm.append((s * parts + r, s_to * parts + r_to))
        return lax.ppermute(a, AXES, perm)

    def other_core(a):
        return send(a, lambda s, r: (s ^ 1, r))

    def along(a, bit):
        return send(a, lambda s, r: (s, r ^ bit))

    def on_device(propagator_matrices, gain, obs_matrix, observations, present, initial, smoother_gain):
        epochs, part_rows, width = propagator_matrices.shape
        place, part = lax.axis_index("slab"), lax.axis_index("row")
        plane, odd = place // 2, place % 2 == 1

        weights = present.astype(jnp.float32)
        drive = weights[:, None] * by(gain, observations)
        taken = lax.optimization_barrier([-weights[e] * gain for e in range(epochs)])

        share = part_rows // 4
        own_share = lax.dynamic_slice_in_dim(smoother_gain, place % 4 * share, share, 0)
        own_share = after(own_share, drive)

        if parts == 4:
            from_x, from_y = along(propagator_matrices, 1), along(propagator_matrices, 2)
            shares = [own_share] + [along(own_share, bit) for bit in (1, 2, 3)]
            shares = jnp.stack(in_order(shares, part), 0)
            mid = epochs // 2
            far = lax.concatenate([along(from_y[:mid], 1), along(from_x[mid:], 2)], 0)
            far = after(far, shares)
            pieces = [propagator_matrices, from_x, from_y, far]
            full = lax.concatenate(in_order(pieces, part), 1)
        else:
            full = lax.all_gather(propagator_matrices, "row", axis=1, tiled=True)
            shares = lax.all_gather(own_share, "row", axis=0)
        next_shares = send(shares, lambda s, r: (s ^ 2, r))

        maps, seen = [], []
        for e in range(epochs):
            reach = mm(full[e], maps[-1]) if e else full[e]
            seen.append(rowwise(mm(obs_matrix, reach)))
            maps.append(reach + mm(taken[e], seen[e]))
        slab_map, shares, next_shares = lax.optimization_barrier((maps[-1], shares, next_shares))
        maps[-1] = slab_map
        else_map = other_core(slab_map)
        mine = jnp.stack(in_order([shares, next_shares], plane % 2), 0)
        theirs = other_core(mine)

        offsets = [after(drive, slab_map)[0:1]]
        seen_0 = [jnp.zeros((1, obs_matrix.shape[0]), jnp.float32)]
        for e in range(1, epochs):
            reach_0 = by(full[e], offsets[-1])
            seen_0.append(by(obs_matrix, reach_0))
            offsets.append(reach_0 + by(taken[e], seen_0[e]) + drive[e : e + 1])
        slab_offset = offsets[-1]

        else_offset = other_core(slab_offset)
        plane_map = mm(jnp.where(odd, slab_map, else_map), jnp.where(odd, else_map, slab_map))
        last_offset = by(slab_map, else_offset) + slab_offset
        else_last = after(other_core(last_offset), plane_map)
        plane_offset = jnp.where(odd, last_offset, else_last)

        powers = []
        count = 2 * epochs * planes

        def first_work(ahead):
            smoother = jnp.stack(in_order(after([mine, theirs], ahead), place % 2), 1)
            powers.append(smoother.transpose(2, 0, 1, 3, 4).reshape(width, width))
            powers.append(mm(powers[0], powers[0]))
            maps_0, base = after((seen, seen_0), ahead)
            seen[:] = [
                lax.concatenate([-weights[e] * maps_0[e] for e in range(epochs)], 0),
                weights[:, None] * (observations - lax.concatenate(base, 0)),
            ]

        def second_work(ahead):
            powers[-1], seen[:] = after((powers[-1], seen), ahead)
            powers.append(mm(powers[-1], powers[-1]))
            moved = [rowwise(mm(seen[0], else_map)), by(seen[0], else_offset).reshape(seen[1].shape) + seen[1]]
            seen[:] = [jnp.where(odd, a, b) for a, b in zip(moved, seen)]
            seen.extend([other_core(a) for a in seen])

        def third_work(ahead):
            powers[-1], seen[:] = after((powers[-1], seen), ahead)
            seen[:] = [
                lax.concatenate(in_order(list(a), place % 2), 0) for a in zip(seen[:2], seen[2:])
            ]
            while 2 ** len(powers) < count:
                powers.append(mm(powers[-1], powers[-1]))

        works = [first_work, second_work, third_work]
        state = initial[None, :]
        for k in range(planes - 1):
            ahead = by(plane_map, state) + plane_offset
            received = send(ahead, lambda s, r: (s + 2, r), lambda s: s // 2 == k)
            if works:
                works.pop(0)(ahead)
                received, powers, seen = lax.optimization_barrier((received, powers, seen))
            state = jnp.where(plane == k + 1, received, state)
        for work in works:
            work(state)

        innovations = by(seen[0], state).reshape(seen[1].shape) + seen[1]
        own = by(gain, innovations)
        terms = [own]
        for k in range(1, planes):
            terms.append(send(own, lambda s, r: (s - 2 * k, r)))

        state = after(state, own)
        state = jnp.where(odd, by(else_map, state) + else_offset, state)
        correction = jnp.where(odd, own[epochs:], own[:epochs])
        filtered = lax.concatenate([by(maps[e], state) + offsets[e] for e in range(epochs)], 0)

        carried = lax.concatenate(terms, 0)
        for i, power in enumerate(powers):
            later = jnp.pad(carried[2**i :], ((0, 2**i), (0, 0)))
            carried = carried + by(power, later)
        carried = jnp.where(odd, carried[epochs : 2 * epochs], carried[:epochs])
        return (filtered, filtered + carried - correction)

    placed = (P("slab", "row", None), P(), P(), P("slab", None), P("slab"), P(), P("row", None))
    return jax.shard_map(
        on_device,
        mesh=mesh,
        in_specs=placed,
        out_specs=(P("slab", None), P("slab", None)),
        check_vma=False,
    )
```
